32 devices in a mesh: leaf: 8 (over z, x), row: 2 (over y), col: 2 (over core).
Axes of the slice: x: 2, y: 2, z: 4, core: 2. Of those that a mesh axis runs over, the one named last changes fastest.
Arguments:
- leaf_rhs: bfloat16 [8, 4096, 128], P('leaf', ('row', 'col')), may hold values from -6 to 6
- leaf_factor: bfloat16 [8, 4096, 4096], P('leaf', ('row', 'col')), as said below
- leaf_coupling: bfloat16 [8, 4096, 4096], P('leaf', None, ('row', 'col')), may hold values from -0.046875 to 0.046875
- border_rows: int32 [8, 4096], P('leaf'), may hold values from 0 to 4095, as said below
- border_count: int32 [8], P('leaf'), may hold values from 1024 to 4096, as said below
- separator_rhs: bfloat16 [4096, 128], P(('leaf', 'row', 'col')), may hold values from -6 to 6
- separator_factor: bfloat16 [4096, 4096], P(('leaf', 'row', 'col')), as said below
Outputs:
- leaf_solution: float32 [8, 4096, 128], P('leaf', ('row', 'col'))
- separator_solution: float32 [4096, 128], P(('leaf', 'row', 'col'))
The draws below stay inside these ranges and needn't reach their ends.
Inputs may be any that keep to these rules, and one draw needn't show every extreme that they name: `border_rows`: the 4096 row numbers of one section are distinct. Border rows j < border_count[k] of section k are live, the others are unused; some section has all 4096 live. `leaf_factor`: lower triangular with a positive diagonal. `separator_factor`: lower triangular with a positive diagonal.
All inputs are finite; a program needn't handle non-finite values.
Results may differ from the reference program's by a relative error of at most 0.013.
Values may be sent and summed in bfloat16 or wider, within the bound.
No kernel may reach another device: no remote copies, remote signals or barrier semaphores. Data moves between devices by JAX's collectives and lax.ppermute only.
A program may use at most 64 MiB of HBM per device.

```python
import jax
import jax.numpy as jnp
from jax import lax

F = 4096
B = 4096
S = 4096
R = 128
SECTIONS = 8


def lower_factor(key, leading, order):
    first, second = jax.random.split(key)
    shape = leading + (order, order)
    diagonal = jax.random.uniform(first, leading + (order,), jnp.float32, 0.6, 1.4)
    spread = jax.random.normal(second, shape, jnp.float32)
    spread = spread / jnp.sqrt(jnp.float32(order))
    row_index = jnp.arange(order)[:, None]
    col_index = jnp.arange(order)[None, :]
    below = row_index > col_index
    same = row_index == col_index
    return jnp.where(below, spread, 0.0) + jnp.where(same, diagonal[..., :, None], 0.0)


def draw_leaf_factor(key, part):
    return lower_factor(key, (SECTIONS,), F).astype(jnp.bfloat16)


def draw_separator_factor(key, part):
    return lower_factor(key, (), S).astype(jnp.bfloat16)


def pick_rows(single):
    return jax.random.permutation(single, S)[:B]


def draw_border_rows(key, part):
    keys = jax.random.split(jax.random.fold_in(key, 11), SECTIONS)
    return jax.vmap(pick_rows)(keys).astype(jnp.int32)


def draw_border_count(key, part):
    first, second = jax.random.split(jax.random.fold_in(key, 23))
    counts = jax.random.randint(first, (SECTIONS,), B // 4, B + 1)
    chosen = jax.random.randint(second, (), 0, SECTIONS)
    return jnp.where(jnp.arange(SECTIONS) == chosen, B, counts).astype(jnp.int32)


def block_scale(key, dims, shards, least, high):
    level, own = 1.0, jax.random.fold_in(key, 6)
    for dim, parts in shards:
        steps = jnp.exp(jax.random.uniform(jax.random.fold_in(own, dim), (parts,), jnp.float32, least / len(shards), high / len(shards)))
        level = level * jnp.repeat(steps, dims[dim] // parts).reshape([-1 if axis == dim else 1 for axis in range(len(dims))])
    return level


def scatter_about(rng, shape, scale, most, cuts=(), held_as=jnp.bfloat16):
    array = jax.random.normal(rng, shape, jnp.float32) * scale
    if len(cuts) > 0:
        array = block_scale(rng, shape, cuts, -0.22, 0.18) * array
    return jnp.clip(array, min=-most, max=most).astype(held_as)


def setup_inputs(seed: int = 0) -> dict:
    seeds = jax.random.split(jax.random.key(seed), 8)
    return {
        "leaf_rhs": scatter_about(seeds[0], (SECTIONS, F, R), 1.0, 6.0, ((0, 8), (1, 4))),
        "leaf_factor": draw_leaf_factor(jax.random.fold_in(seeds[7], 71), 0),
        "leaf_coupling": scatter_about(seeds[2], (SECTIONS, B, F), (4 * F) ** -0.5, 0.046875, ((0, 8), (2, 4))),
        "border_rows": draw_border_rows(jax.random.fold_in(seeds[7], 71), 0),
        "border_count": draw_border_count(jax.random.fold_in(seeds[7], 71), 0),
        "separator_rhs": scatter_about(seeds[5], (S, R), 1.0, 6.0, ((0, 32),)),
        "separator_factor": draw_separator_factor(jax.random.fold_in(seeds[7], 71), 0),
    }


def reference(leaf_rhs, leaf_factor, leaf_coupling, border_rows, border_count, separator_rhs, separator_factor):
    positions = jnp.arange(B, dtype=jnp.int32)

    def descend(carry, inputs):
        rhs_block, factor, coupling, index_set, count = inputs
        forward = jnp.dot(factor, rhs_block, preferred_element_type=jnp.float32).astype(jnp.bfloat16)
        update = jnp.dot(coupling, forward, preferred_element_type=jnp.float32)
        update = jnp.where((positions < count)[:, None], update, jnp.zeros((), update.dtype))
        return carry.at[index_set].add(-update), forward

    gathered, forwards = lax.scan(descend, separator_rhs.astype(jnp.float32), (leaf_rhs, leaf_factor, leaf_coupling, border_rows, border_count))
    root_forward = jnp.dot(separator_factor, gathered.astype(jnp.bfloat16), preferred_element_type=jnp.float32).astype(jnp.bfloat16)
    separator_solution = jnp.dot(separator_factor.T, root_forward, preferred_element_type=jnp.float32)
    rounded = separator_solution.astype(jnp.bfloat16)

    def ascend(inputs):
        forward, factor, coupling, index_set, count = inputs
        border = jnp.where((positions < count)[:, None], rounded[index_set], jnp.zeros((), rounded.dtype))
        corrected = (forward.astype(jnp.float32) - jnp.dot(coupling.T, border, preferred_element_type=jnp.float32)).astype(jnp.bfloat16)
        return jnp.dot(factor.T, corrected, preferred_element_type=jnp.float32)

    leaf_solution = lax.map(ascend, (forwards, leaf_factor, leaf_coupling, border_rows, border_count))
    return leaf_solution, separator_solution
```

```python
import functools

import jax
import jax.numpy as jnp
from jax import lax
from jax.experimental import pallas as pl
from jax.experimental.pallas import tpu as pltpu
from jax.sharding import PartitionSpec as P

BF16 = jnp.bfloat16
F32 = jnp.float32
AXES = ("leaf", "row", "col")
FIRST = (((0,), (0,)), ((), ()))
VM = pl.BlockSpec(memory_space=pltpu.VMEM)
SM = pl.BlockSpec(memory_space=pltpu.SMEM)
UNROLL = 64


def kernel_call(body, outs, operands, scratch=(), flops=0, vmem=24, name=None):
    moved = sum(a.size * a.dtype.itemsize for a in operands)
    moved += sum(o.size * o.dtype.itemsize for o in outs)
    specs = [SM if a.dtype == jnp.int32 else VM for a in operands]
    return pl.pallas_call(
        body,
        out_shape=list(outs),
        in_specs=specs,
        out_specs=[VM] * len(outs),
        scratch_shapes=list(scratch),
        name=name,
        cost_estimate=pl.CostEstimate(flops=flops, bytes_accessed=moved, transcendentals=0),
        compiler_params=pltpu.CompilerParams(vmem_limit_bytes=vmem << 20),
    )(*operands)


def forward_kernel(blocks, index, factor, *refs):
    pieces, out = refs[:-1], refs[-1]
    rows = factor.shape[0]
    total = None
    for k in range(blocks):
        start = pl.multiple_of(index[k] * rows, rows)
        term = jnp.dot(factor[:, pl.ds(start, rows)], pieces[k][...], preferred_element_type=F32)
        total = term if total is None else total + term
    out[...] = total.astype(BF16)


def chunk_of(rows):
    return 512 if rows % 512 == 0 else rows


def update_kernel(groups, place, coupling, forward, *refs):
    own, sent, placed, held = refs[0], refs[1:groups], refs[groups], refs[groups + 1]
    order = placed.shape[0] - 8
    borders = coupling.shape[0]
    step = chunk_of(borders)
    placed[...] = jnp.zeros_like(placed)
    value = forward[...]
    for first in range(0, borders, step):
        held[...] = jnp.dot(
            coupling[first : first + step, :], value, preferred_element_type=F32
        )

        def body(i, _):
            base = i * UNROLL
            for t in range(UNROLL):
                placed[pl.ds(place[first + base + t], 1), :] = held[pl.ds(base + t, 1), :]
            return 0

        lax.fori_loop(0, step // UNROLL, body, 0)
    part = order // groups
    own[...] = placed[0:part, :]
    for k, ref in enumerate(sent):
        ref[...] = placed[(k + 1) * part : (k + 2) * part, :].astype(BF16)


def add_kernel(arrived, parts, *refs):
    own, received = refs[0], refs[1 : 1 + arrived]
    kept, sent = refs[1 + arrived], refs[2 + arrived :]
    rows = own.shape[0] // parts
    for k in range(parts):
        span = slice(k * rows, (k + 1) * rows)
        total = own[span, :]
        for ref in received:
            total = total + ref[span, :].astype(F32)
        if k == 0:
            kept[...] = total
        else:
            sent[k - 1][...] = total.astype(BF16)


def gathered_kernel(arrived, *refs):
    rhs, own, received, out = refs[0], refs[1], refs[2 : 2 + arrived], refs[-1]
    total = own[...]
    for ref in received:
        total = total + ref[...].astype(F32)
    out[...] = (rhs[...].astype(F32) - total).astype(BF16)


def finish_kernel(arrived, *refs):
    own, received = refs[0], refs[1 : 1 + arrived]
    total = own[...]
    for ref in received:
        total = total + ref[...].astype(F32)
    refs[-2][...] = total
    refs[-1][...] = total.astype(BF16)


def stack_kernel(*refs):
    out = refs[-1]
    rows = refs[0].shape[0]
    for k, ref in enumerate(refs[:-1]):
        out[k * rows : (k + 1) * rows, :] = ref[...]


def split_kernel(parts, groups, column, factor, *refs):
    size = factor.shape[0]
    for k in range(parts):
        for g in range(groups):
            start = pl.multiple_of(column[k * groups + g] * size, size)
            refs[k][:, g * size : (g + 1) * size] = factor[:, pl.ds(start, size)]


def root_forward_kernel(parts, halves, *refs):
    blocks, right = refs[:parts], refs[parts : parts + halves]
    kept, sent = refs[-2], refs[-1]
    rows = blocks[0].shape[0]
    width = right[0].shape[0]
    for k in range(parts):
        total = None
        for h in range(halves):
            term = jnp.dot(
                blocks[k][:, h * width : (h + 1) * width],
                right[h][...],
                preferred_element_type=F32,
            )
            total = term if total is None else total + term
        kept[k * rows : (k + 1) * rows, :] = total
        sent[k * rows : (k + 1) * rows, :] = total.astype(BF16)


def root_back_kernel(parts, halves, sources, *refs):
    blocks, own = refs[:parts], refs[parts]
    received = refs[parts + 1 : 2 * parts]
    outs = refs[2 * parts :]
    rows = blocks[0].shape[0]
    others = [ref[...].astype(F32) for ref in received]
    values = []
    for k in range(parts):
        total = own[k * rows : (k + 1) * rows, :]
        for other, source in zip(others, sources):
            total = total + other[source[k] * rows : (source[k] + 1) * rows, :]
        values.append(total.astype(BF16))
    width = blocks[0].shape[1] // halves
    for h in range(halves):
        total = None
        for k in range(parts):
            term = lax.dot_general(
                blocks[k][:, h * width : (h + 1) * width],
                values[k],
                FIRST,
                preferred_element_type=F32,
            )
            total = term if total is None else total + term
        outs[h][...] = total.astype(outs[h].dtype)


def border_kernel(blocks, place, index, coupling, factor, forward, *refs):
    pieces = refs[:blocks]
    corrected, sent = refs[blocks], refs[blocks + 1 : -2]
    table, held = refs[-2], refs[-1]
    rows = pieces[0].shape[0]
    order = blocks * rows
    for k in range(blocks):
        table[k * rows : (k + 1) * rows, :] = pieces[k][...].astype(F32)
    table[order : order + 8, :] = jnp.zeros((8, table.shape[1]), F32)
    borders = coupling.shape[0]
    step = chunk_of(borders)
    total = forward[...].astype(F32).T
    for first in range(0, borders, step):

        def body(i, _):
            base = pl.multiple_of(i * UNROLL, UNROLL)
            for t in range(UNROLL):
                held[pl.ds(base + t, 1), :] = table[pl.ds(place[first + base + t], 1), :]
            return 0

        lax.fori_loop(0, step // UNROLL, body, 0)
        total = total - lax.dot_general(
            held[...].astype(BF16),
            coupling[first : first + step, :],
            FIRST,
            preferred_element_type=F32,
        )
    value = total.astype(BF16)
    corrected[...] = value
    width = factor.shape[0]
    for k, ref in enumerate(sent):
        start = pl.multiple_of(index[k] * width, width)
        ref[...] = jnp.dot(
            value, factor[:, pl.ds(start, width)], preferred_element_type=F32
        ).astype(ref.dtype)


def blocks_kernel(index, factor, corrected, *outs):
    width = factor.shape[0]
    for k, ref in enumerate(outs):
        start = pl.multiple_of(index[k] * width, width)
        ref[...] = jnp.dot(
            corrected[...], factor[:, pl.ds(start, width)], preferred_element_type=F32
        ).astype(ref.dtype)


def sum_kernel(out_dtype, *refs):
    total = refs[0][...].astype(F32)
    for ref in refs[1:-1]:
        total = total + ref[...].astype(F32)
    refs[-1][...] = total.astype(out_dtype)


def last_kernel(*refs):
    total = refs[0][...].astype(F32)
    for ref in refs[1:-1]:
        total = total + ref[...].astype(F32)
    refs[-1][...] = total.T


def like(shape, dtype):
    return jax.ShapeDtypeStruct(tuple(shape), dtype)


def local(
    sizes,
    leaf_rhs,
    leaf_factor,
    leaf_coupling,
    border_rows,
    border_count,
    separator_rhs,
    separator_factor,
):
    nl, nr, nc = sizes
    nx = 2 if nl % 2 == 0 else 1
    nz = nl // nx
    rhs, factor, coupling = leaf_rhs[0], leaf_factor[0], leaf_coupling[0]
    rows, columns = rhs.shape
    borders = coupling.shape[0]
    own_rows, order = separator_factor.shape
    leaf = lax.axis_index("leaf")
    z, x = leaf // nx, leaf % nx
    y, c = lax.axis_index("row"), lax.axis_index("col")
    plane = [(dx, dy) for dx in range(nx) for dy in range(nr)]
    parts = len(plane)
    section = [(dy, dc) for dy in range(nr) for dc in range(nc)]

    def shift(value, dz=0, dx=0, dy=0, dc=0):
        pairs = []
        for a in range(nz):
            for b in range(nx):
                for d in range(nr):
                    for e in range(nc):
                        here = ((a * nx + b) * nr + d) * nc + e
                        a2, b2 = (a + dz) % nz, (b + dx) % nx
                        d2, e2 = (d + dy) % nr, (e + dc) % nc
                        pairs.append((here, ((a2 * nx + b2) * nr + d2) * nc + e2))
        return lax.ppermute(value, AXES, pairs)

    by_row = {0: rhs}
    for dy in range(1, nr):
        by_row[dy] = shift(rhs, dy=-dy)
    pieces = []
    for dy, dc in section:
        pieces.append(by_row[dy] if dc == 0 else shift(by_row[dy], dc=-dc))
    block = jnp.stack([((y + dy) % nr) * nc + (c + dc) % nc for dy, dc in section]).astype(
        jnp.int32
    )

    row = border_rows[0]
    device, inside = row // own_rows, row % own_rows
    rel_c = (device % nc - c) % nc
    rel_y = (device // nc % nr - y) % nr
    rel_x = (device // (nc * nr) % nx - x) % nx
    rel_z = (device // (nc * nr * nx) - z) % nz
    place = (((rel_c * nx + rel_x) * nr + rel_y) * nz + rel_z) * own_rows + inside
    live = jnp.arange(borders, dtype=jnp.int32) < border_count[0]
    place = jnp.where(live, place, order).astype(jnp.int32)

    groups = [(dc, dz) for dc in range(nc) for dz in range(nz)]
    wide = len(groups) * own_rows

    def owner(dx, dy, dz, dc):
        return ((((z + dz) % nz) * nx + (x + dx) % nx) * nr + (y + dy) % nr) * nc + (c + dc) % nc

    if own_rows % 128 == 0:
        column = jnp.stack(
            [owner(dx, dy, dz, dc) for dx, dy in plane for dc, dz in groups]
        ).astype(jnp.int32)
        cut = kernel_call(
            functools.partial(split_kernel, parts, len(groups)),
            [like((own_rows, wide), BF16)] * parts,
            [column, separator_factor],
            name="split",
        )
    else:
        cut = [
            jnp.concatenate(
                [
                    lax.dynamic_slice_in_dim(
                        separator_factor, owner(dx, dy, dz, dc) * own_rows, own_rows, 1
                    )
                    for dc, dz in groups
                ],
                1,
            )
            for dx, dy in plane
        ]
    root = [cut[0]]
    for (dx, dy) in plane[1:]:
        k = plane.index(((-dx) % nx, (-dy) % nr))
        root.append(shift(cut[k], dx=-dx, dy=-dy))

    forward = kernel_call(
        functools.partial(forward_kernel, len(section)),
        [like((rows, columns), BF16)],
        [block, factor, *pieces],
        flops=2 * factor.size * columns,
        name="forward",
    )[0]

    half = order // nc
    outs = kernel_call(
        functools.partial(update_kernel, nc),
        [like((half, columns), F32)] + [like((half, columns), BF16)] * (nc - 1),
        [place, coupling, forward],
        scratch=[
            pltpu.VMEM((order + 8, columns), F32),
            pltpu.VMEM((chunk_of(borders), columns), F32),
        ],
        flops=2 * coupling.size * columns,
        name="update",
    )
    received = [shift(outs[dc], dc=dc) for dc in range(1, nc)]
    size = half // parts
    outs = kernel_call(
        functools.partial(add_kernel, len(received), parts),
        [like((size, columns), F32)] + [like((size, columns), BF16)] * (parts - 1),
        [outs[0], *received],
        name="add_col",
    )
    received = [shift(outs[k], dx=plane[k][0], dy=plane[k][1]) for k in range(1, parts)]
    outs = kernel_call(
        functools.partial(add_kernel, len(received), nz),
        [like((own_rows, columns), F32)] + [like((own_rows, columns), BF16)] * (nz - 1),
        [outs[0], *received],
        name="add_plane",
    )
    received = [shift(outs[dz], dz=dz) for dz in range(1, nz)]
    gathered = kernel_call(
        functools.partial(gathered_kernel, len(received)),
        [like((own_rows, columns), BF16)],
        [separator_rhs, outs[0], *received],
        name="gathered",
    )[0]

    def along_z(value):
        values = [value] + [shift(value, dz=-dz) for dz in range(1, nz)]
        return kernel_call(
            stack_kernel, [like((nz * own_rows, columns), BF16)], values, name="stack"
        )[0]

    column_block = along_z(gathered)
    right = [column_block] + [shift(column_block, dc=-dc) for dc in range(1, nc)]
    kept, sent = kernel_call(
        functools.partial(root_forward_kernel, parts, nc),
        [like((parts * own_rows, columns), F32), like((parts * own_rows, columns), BF16)],
        [*root, *right],
        flops=2 * parts * own_rows * wide * columns,
        name="root_forward",
    )
    received, sources = [], []
    for dx, dy in plane[1:]:
        received.append(shift(sent, dx=-dx, dy=-dy))
        sources.append([plane.index(((px - dx) % nx, (py - dy) % nr)) for px, py in plane])
    outs = kernel_call(
        functools.partial(root_back_kernel, parts, nc, sources),
        [like((nz * own_rows, columns), F32)] + [like((nz * own_rows, columns), BF16)] * (nc - 1),
        [*root, kept, *received],
        flops=2 * parts * own_rows * wide * columns,
        name="root_back",
    )
    received = [shift(outs[dc], dc=dc) for dc in range(1, nc)]
    outs = kernel_call(
        functools.partial(add_kernel, len(received), nz),
        [like((own_rows, columns), F32)] + [like((own_rows, columns), BF16)] * (nz - 1),
        [outs[0], *received],
        name="add_col2",
    )
    received = [shift(outs[dz], dz=dz) for dz in range(1, nz)]
    separator_solution, rounded = kernel_call(
        functools.partial(finish_kernel, len(received)),
        [like((own_rows, columns), F32), like((own_rows, columns), BF16)],
        [outs[0], *received],
        name="finish",
    )
    layer = along_z(rounded)
    table = [layer] + [shift(layer, dx=-dx, dy=-dy) for dx, dy in plane[1:]]
    pieces = list(table)
    for dc in range(1, nc):
        pieces += [shift(value, dc=-dc) for value in table]

    far = [(dy, dc) for dy, dc in section if dy > 0]
    near = [(dy, dc) for dy, dc in section if dy == 0]
    far_block = block[nc:]
    near_block = block[:nc]
    outs = kernel_call(
        functools.partial(border_kernel, len(pieces)),
        [like((columns, rows), BF16)]
        + [like((columns, rows), F32 if dc == 0 else BF16) for dy, dc in far],
        [place, far_block, coupling, factor, forward, *pieces],
        scratch=[
            pltpu.VMEM((order + 8, columns), F32),
            pltpu.VMEM((chunk_of(borders), columns), F32),
        ],
        flops=2 * (coupling.size + factor.size * len(far) // len(section)) * columns,
        name="border",
    )
    corrected, far_parts = outs[0], dict(zip(far, outs[1:]))
    arrived = []
    for dy in range(1, nr):
        terms = [far_parts[dy, 0]] + [shift(far_parts[dy, dc], dc=dc) for dc in range(1, nc)]
        total = kernel_call(
            functools.partial(sum_kernel, BF16), [like((columns, rows), BF16)], terms, name="sum_far"
        )[0]
        arrived.append(shift(total, dy=dy))
    outs = kernel_call(
        blocks_kernel,
        [like((columns, rows), F32 if dc == 0 else BF16) for dy, dc in near],
        [near_block, factor, corrected],
        flops=2 * factor.size * len(near) // len(section) * columns,
        name="near",
    )
    terms = [outs[0]] + [shift(outs[dc], dc=dc) for dc in range(1, nc)]
    leaf_solution = kernel_call(
        last_kernel, [like((rows, columns), F32)], [*terms, *arrived], name="last"
    )[0]
    return leaf_solution[None], separator_solution


def solution(mesh):
    sizes = tuple(mesh.shape[name] for name in AXES)
    placed = (
        P("leaf", ("row", "col"), None),
        P("leaf", ("row", "col"), None),
        P("leaf", None, ("row", "col")),
        P("leaf", None),
        P("leaf"),
        P(AXES, None),
        P(AXES, None),
    )
    return jax.shard_map(
        functools.partial(local, sizes),
        mesh=mesh,
        in_specs=placed,
        out_specs=(P("leaf", ("row", "col"), None), P(AXES, None)),
        check_vma=False,
    )
```

```python
import functools

import jax
import jax.numpy as jnp
from jax import lax
from jax.experimental import pallas as pl
from jax.experimental.pallas import tpu as pltpu
from jax.sharding import PartitionSpec as P


BF16 = jnp.bfloat16
F32 = jnp.float32
AXES = ("leaf", "row", "col")
FIRST = (((0,), (0,)), ((), ()))
VM = pl.BlockSpec(memory_space=pltpu.VMEM)
SM = pl.BlockSpec(memory_space=pltpu.SMEM)
ANY = pl.BlockSpec(memory_space=pltpu.HBM)


def kernel_call(body, outs, operands, scratch=(), flops=0, vmem=10, apart=()):
    moved = sum(a.size * a.dtype.itemsize for a in operands)
    moved += sum(o.size * o.dtype.itemsize for o in outs)
    specs = [
        ANY if k in apart else SM if a.dtype == jnp.int32 else VM for k, a in enumerate(operands)
    ]
    return pl.pallas_call(
        body,
        out_shape=list(outs),
        in_specs=specs,
        out_specs=[VM] * len(outs),
        scratch_shapes=list(scratch),
        cost_estimate=pl.CostEstimate(flops=flops, bytes_accessed=moved, transcendentals=0),
        compiler_params=pltpu.CompilerParams(vmem_limit_bytes=vmem << 20),
    )(*operands)


def load_kernel(section, parts, groups, block, column, factor, coupling, separator, *refs):
    wide, tall, cut, sems = refs[:section], refs[section], refs[section + 1 : -1], refs[-1]
    width, size = factor.shape[0], separator.shape[0]
    copies = []
    for k in range(section):
        start = pl.multiple_of(block[k] * width, width)
        copies.append(
            pltpu.make_async_copy(factor.at[:, pl.ds(start, width)], wide[k], sems.at[k])
        )
    for k in range(parts):
        for g in range(groups):
            start = pl.multiple_of(column[k * groups + g] * size, size)
            copies.append(
                pltpu.make_async_copy(
                    separator.at[:, pl.ds(start, size)],
                    cut[k].at[:, pl.ds(g * size, size)],
                    sems.at[len(copies)],
                )
            )
    copies.append(pltpu.make_async_copy(coupling, tall, sems.at[len(copies)]))
    for copy in copies:
        copy.start()
    for copy in copies:
        copy.wait()


def near_kernel(count, *refs):
    blocks, pieces, partial = refs[:count], refs[count : 2 * count], refs[-1]
    total = None
    for k in range(count):
        term = jnp.dot(blocks[k][...], pieces[k][...], preferred_element_type=F32)
        total = term if total is None else total + term
    partial[...] = total


def chunk_of(rows):
    return 256 if rows % 256 == 0 else rows


def update_kernel(groups, far, place, partial, coupling, *refs):
    blocks, pieces = refs[:far], refs[far : 2 * far]
    forward, own, sent = refs[2 * far], refs[2 * far + 1], refs[2 * far + 2 : -3]
    placed, held = refs[-3], refs[-2:]
    order = placed.shape[0] - 8
    borders = coupling.shape[0]
    step = chunk_of(borders)
    count = borders // step
    total = partial[...]
    for k in range(far):
        total = total + jnp.dot(blocks[k][...], pieces[k][...], preferred_element_type=F32)
    forward[...] = total.astype(BF16)
    placed[...] = jnp.zeros_like(placed)

    def multiply(k):
        held[k % 2][...] = jnp.dot(
            coupling[k * step : (k + 1) * step, :], forward[...], preferred_element_type=F32
        )

    def scatter(k):
        for t in range(step):
            placed[pl.ds(place[k * step + t], 1), :] = held[k % 2][t : t + 1, :]

    multiply(0)
    for k in range(count):
        if k + 1 < count:
            multiply(k + 1)
        scatter(k)
    part = order // groups
    own[...] = placed[0:part, :]
    for k, ref in enumerate(sent):
        ref[...] = placed[(k + 1) * part : (k + 2) * part, :].astype(BF16)


def add_kernel(arrived, parts, *refs):
    own, received = refs[0], refs[1 : 1 + arrived]
    kept, sent = refs[1 + arrived], refs[2 + arrived :]
    rows = own.shape[0] // parts
    for k in range(parts):
        span = slice(k * rows, (k + 1) * rows)
        total = own[span, :]
        for ref in received:
            total = total + ref[span, :].astype(F32)
        if k == 0:
            kept[...] = total
        else:
            sent[k - 1][...] = total.astype(BF16)


def gathered_kernel(arrived, *refs):
    rhs, own, received, out = refs[0], refs[1], refs[2 : 2 + arrived], refs[-1]
    total = own[...]
    for ref in received:
        total = total + ref[...].astype(F32)
    out[...] = (rhs[...].astype(F32) - total).astype(BF16)


def finish_kernel(arrived, *refs):
    own, received = refs[0], refs[1 : 1 + arrived]
    total = own[...]
    for ref in received:
        total = total + ref[...].astype(F32)
    refs[-2][...] = total
    refs[-1][...] = total.astype(BF16)


def stack_kernel(*refs):
    out = refs[-1]
    rows = refs[0].shape[0]
    for k, ref in enumerate(refs[:-1]):
        out[k * rows : (k + 1) * rows, :] = ref[...]


def root_forward_kernel(parts, halves, *refs):
    blocks, right = refs[:parts], refs[parts : parts + halves]
    kept, sent = refs[-2], refs[-1]
    rows = blocks[0].shape[0]
    width = right[0].shape[0]
    for k in range(parts):
        total = None
        for h in range(halves):
            term = jnp.dot(
                blocks[k][:, h * width : (h + 1) * width],
                right[h][...],
                preferred_element_type=F32,
            )
            total = term if total is None else total + term
        kept[k * rows : (k + 1) * rows, :] = total
        sent[k * rows : (k + 1) * rows, :] = total.astype(BF16)


def root_back_kernel(parts, halves, sources, *refs):
    blocks, own = refs[:parts], refs[parts]
    received = refs[parts + 1 : 2 * parts]
    outs = refs[2 * parts :]
    rows = blocks[0].shape[0]
    others = [ref[...].astype(F32) for ref in received]
    values = []
    for k in range(parts):
        total = own[k * rows : (k + 1) * rows, :]
        for other, source in zip(others, sources):
            total = total + other[source[k] * rows : (source[k] + 1) * rows, :]
        values.append(total.astype(BF16))
    width = blocks[0].shape[1] // halves
    for h in range(halves):
        total = None
        for k in range(parts):
            term = lax.dot_general(
                blocks[k][:, h * width : (h + 1) * width],
                values[k],
                FIRST,
                preferred_element_type=F32,
            )
            total = term if total is None else total + term
        outs[h][...] = total.astype(outs[h].dtype)


def border_kernel(blocks, far, place, forward, coupling, *refs):
    wide, pieces = refs[:far], refs[far : far + blocks]
    corrected, sent = refs[far + blocks], refs[far + blocks + 1 : -4]
    table, sums, held = refs[-4], refs[-3], refs[-2:]
    rows = pieces[0].shape[0]
    order = blocks * rows
    borders = coupling.shape[0]
    step = chunk_of(borders)
    count = borders // step
    for k in range(blocks):
        table[k * rows : (k + 1) * rows, :] = pieces[k][...].astype(F32)
    table[order : order + 8, :] = jnp.zeros((8, table.shape[1]), F32)
    sums[...] = forward[...].astype(F32).T

    def gather(k):
        for t in range(step):
            held[k % 2][t : t + 1, :] = table[pl.ds(place[k * step + t], 1), :]

    def multiply(k):
        sums[...] -= lax.dot_general(
            held[k % 2][...].astype(BF16),
            coupling[k * step : (k + 1) * step, :],
            FIRST,
            preferred_element_type=F32,
        )

    gather(0)
    for k in range(count):
        if k + 1 < count:
            gather(k + 1)
        multiply(k)
    corrected[...] = sums[...].astype(BF16)
    for k, ref in enumerate(sent):
        ref[...] = jnp.dot(
            corrected[...], wide[k][...], preferred_element_type=F32
        ).astype(ref.dtype)


def blocks_kernel(corrected, *refs):
    count = len(refs) // 2
    for wide, ref in zip(refs[:count], refs[count:]):
        ref[...] = jnp.dot(
            corrected[...], wide[...], preferred_element_type=F32
        ).astype(ref.dtype)


def sum_kernel(out_dtype, *refs):
    total = refs[0][...].astype(F32)
    for ref in refs[1:-1]:
        total = total + ref[...].astype(F32)
    refs[-1][...] = total.astype(out_dtype)


def last_kernel(*refs):
    total = refs[0][...].astype(F32)
    for ref in refs[1:-1]:
        total = total + ref[...].astype(F32)
    refs[-1][...] = total.T


def like(shape, dtype):
    return jax.ShapeDtypeStruct(tuple(shape), dtype)


def local(
    sizes,
    leaf_rhs,
    leaf_factor,
    leaf_coupling,
    border_rows,
    border_count,
    separator_rhs,
    separator_factor,
):
    nl, nr, nc = sizes
    nx = 2 if nl % 2 == 0 else 1
    nz = nl // nx
    rhs, factor, coupling = leaf_rhs[0], leaf_factor[0], leaf_coupling[0]
    rows, columns = rhs.shape
    borders = coupling.shape[0]
    own_rows, order = separator_factor.shape
    leaf = lax.axis_index("leaf")
    z, x = leaf // nx, leaf % nx
    y, c = lax.axis_index("row"), lax.axis_index("col")
    plane = [(dx, dy) for dx in range(nx) for dy in range(nr)]
    parts = len(plane)
    section = [(dy, dc) for dy in range(nr) for dc in range(nc)]

    def shift(value, dz=0, dx=0, dy=0, dc=0):
        pairs = []
        for a in range(nz):
            for b in range(nx):
                for d in range(nr):
                    for e in range(nc):
                        here = ((a * nx + b) * nr + d) * nc + e
                        a2, b2 = (a + dz) % nz, (b + dx) % nx
                        d2, e2 = (d + dy) % nr, (e + dc) % nc
                        pairs.append((here, ((a2 * nx + b2) * nr + d2) * nc + e2))
        return lax.ppermute(value, AXES, pairs)

    def send_z(values):
        out = []
        for dz in range(1, nz):
            out.append(shift(values[dz], dz=dz))
        return out

    by_row = {0: rhs}
    for dy in range(1, nr):
        by_row[dy] = shift(rhs, dy=-dy)
    pieces = []
    for dy, dc in section:
        pieces.append(by_row[dy] if dc == 0 else shift(by_row[dy], dc=-dc))
    block = jnp.stack([((y + dy) % nr) * nc + (c + dc) % nc for dy, dc in section]).astype(
        jnp.int32
    )

    row = border_rows[0]
    device, inside = row // own_rows, row % own_rows
    rel_c = (device % nc - c) % nc
    rel_y = (device // nc % nr - y) % nr
    rel_x = (device // (nc * nr) % nx - x) % nx
    rel_z = (device // (nc * nr * nx) - z) % nz
    place = (((rel_c * nx + rel_x) * nr + rel_y) * nz + rel_z) * own_rows + inside
    live = jnp.arange(borders, dtype=jnp.int32) < border_count[0]
    place = jnp.where(live, place, order).astype(jnp.int32)

    groups = [(dc, dz) for dc in range(nc) for dz in range(nz)]
    wide = len(groups) * own_rows

    def owner(dx, dy, dz, dc):
        return ((((z + dz) % nz) * nx + (x + dx) % nx) * nr + (y + dy) % nr) * nc + (c + dc) % nc

    direct = own_rows % 128 == 0
    column = jnp.stack(
        [owner(dx, dy, dz, dc) for dx, dy in plane for dc, dz in groups]
    ).astype(jnp.int32)
    loads = parts if direct else 0
    loaded = kernel_call(
        functools.partial(load_kernel, len(section), loads, len(groups)),
        [like((rows, rows), BF16)] * len(section)
        + [like(coupling.shape, BF16)]
        + [like((own_rows, wide), BF16)] * loads,
        [block, column, factor, coupling, separator_factor],
        scratch=[pltpu.SemaphoreType.DMA((len(section) + loads * len(groups) + 1,))],
        vmem=33,
        apart=(2, 3, 4),
    )
    wide_blocks, tall, cut = loaded[: len(section)], loaded[len(section)], loaded[-parts:]
    if not direct:
        cut = [
            jnp.concatenate(
                [
                    lax.dynamic_slice_in_dim(
                        separator_factor, owner(dx, dy, dz, dc) * own_rows, own_rows, 1
                    )
                    for dc, dz in groups
                ],
                1,
            )
            for dx, dy in plane
        ]
    root = [cut[0]]
    held = list(cut)
    late = [plane.index((dx, dy)) for dx, dy in plane if dy > 0]
    if nr > 1:
        *after, pieces[nc] = lax.optimization_barrier((*[cut[k] for k in late], pieces[nc]))
        for k, value in zip(late, after):
            held[k] = value
    for dx, dy in plane[1:]:
        k = plane.index(((-dx) % nx, (-dy) % nr))
        root.append(shift(held[k], dx=-dx, dy=-dy))

    half = order // nc
    far_count = len(section) - nc
    near = kernel_call(
        functools.partial(near_kernel, nc),
        [like((rows, columns), F32)],
        [*wide_blocks[:nc], *pieces[:nc]],
        flops=2 * rows * rows * nc * columns,
    )[0]
    outs = kernel_call(
        functools.partial(update_kernel, nc, far_count),
        [like((rows, columns), BF16), like((half, columns), F32)]
        + [like((half, columns), BF16)] * (nc - 1),
        [place, near, tall, *wide_blocks[nc:], *pieces[nc:]],
        scratch=[pltpu.VMEM((order + 8, columns), F32)]
        + [pltpu.VMEM((chunk_of(borders), columns), F32)] * 2,
        flops=2 * (coupling.size + rows * rows * far_count) * columns,
    )
    forward, outs = outs[0], outs[1:]
    received = [shift(outs[dc], dc=dc) for dc in range(1, nc)]
    size = half // parts
    outs = kernel_call(
        functools.partial(add_kernel, len(received), parts),
        [like((size, columns), F32)] + [like((size, columns), BF16)] * (parts - 1),
        [outs[0], *received],
    )
    received = []
    for k, (dx, dy) in list(enumerate(plane))[1:]:
        received.append(shift(outs[k], dx=dx, dy=dy))
    outs = kernel_call(
        functools.partial(add_kernel, len(received), nz),
        [like((own_rows, columns), F32)] + [like((own_rows, columns), BF16)] * (nz - 1),
        [outs[0], *received],
    )
    received = send_z(outs)
    gathered = kernel_call(
        functools.partial(gathered_kernel, len(received)),
        [like((own_rows, columns), BF16)],
        [separator_rhs, outs[0], *received],
    )[0]

    def along_z(value):
        values = [value]
        for dz in range(1, nz):
            values.append(shift(value, dz=-dz))
        return kernel_call(stack_kernel, [like((nz * own_rows, columns), BF16)], values)[0]

    column_block = along_z(gathered)
    right = [column_block] + [shift(column_block, dc=-dc) for dc in range(1, nc)]
    kept, sent = kernel_call(
        functools.partial(root_forward_kernel, parts, nc),
        [like((parts * own_rows, columns), F32), like((parts * own_rows, columns), BF16)],
        [*root, *right],
        flops=2 * parts * own_rows * wide * columns,
    )
    received, sources = [], []
    for k, (dx, dy) in list(enumerate(plane))[1:]:
        received.append(shift(sent, dx=-dx, dy=-dy))
        sources.append([plane.index(((px - dx) % nx, (py - dy) % nr)) for px, py in plane])
    outs = kernel_call(
        functools.partial(root_back_kernel, parts, nc, sources),
        [like((nz * own_rows, columns), F32)] + [like((nz * own_rows, columns), BF16)] * (nc - 1),
        [*root, kept, *received],
        flops=2 * parts * own_rows * wide * columns,
    )
    received = [shift(outs[dc], dc=dc) for dc in range(1, nc)]
    outs = kernel_call(
        functools.partial(add_kernel, len(received), nz),
        [like((own_rows, columns), F32)] + [like((own_rows, columns), BF16)] * (nz - 1),
        [outs[0], *received],
    )
    received = send_z(outs)
    separator_solution, rounded = kernel_call(
        functools.partial(finish_kernel, len(received)),
        [like((own_rows, columns), F32), like((own_rows, columns), BF16)],
        [outs[0], *received],
    )
    layer = along_z(rounded)
    table = [layer]
    for k, (dx, dy) in list(enumerate(plane))[1:]:
        table.append(shift(layer, dx=-dx, dy=-dy))
    pieces = list(table)
    for dc in range(1, nc):
        pieces += [shift(value, dc=-dc) for value in table]

    far = [(dy, dc) for dy, dc in section if dy > 0]
    near = [(dy, dc) for dy, dc in section if dy == 0]
    outs = kernel_call(
        functools.partial(border_kernel, len(pieces), len(far)),
        [like((columns, rows), BF16)]
        + [like((columns, rows), F32 if dc == 0 else BF16) for dy, dc in far],
        [place, forward, tall, *wide_blocks[nc:], *pieces],
        scratch=[pltpu.VMEM((order + 8, columns), F32), pltpu.VMEM((columns, rows), F32)]
        + [pltpu.VMEM((chunk_of(borders), columns), F32)] * 2,
        flops=2 * (coupling.size + factor.size * len(far) // len(section)) * columns,
    )
    corrected, far_parts = outs[0], dict(zip(far, outs[1:]))
    arrived = []
    for dy in range(1, nr):
        terms = [far_parts[dy, 0]] + [shift(far_parts[dy, dc], dc=dc) for dc in range(1, nc)]
        total = kernel_call(
            functools.partial(sum_kernel, BF16), [like((columns, rows), BF16)], terms
        )[0]
        arrived.append(shift(total, dy=dy))
    outs = kernel_call(
        blocks_kernel,
        [like((columns, rows), F32 if dc == 0 else BF16) for dy, dc in near],
        [corrected, *wide_blocks[:nc]],
        flops=2 * factor.size * len(near) // len(section) * columns,
    )
    terms = [outs[0]] + [shift(outs[dc], dc=dc) for dc in range(1, nc)]
    leaf_solution = kernel_call(last_kernel, [like((rows, columns), F32)], [*terms, *arrived])[0]
    return leaf_solution[None], separator_solution


def solution(mesh):
    sizes = tuple(mesh.shape[name] for name in AXES)
    placed = (
        P("leaf", ("row", "col"), None),
        P("leaf", ("row", "col"), None),
        P("leaf", None, ("row", "col")),
        P("leaf", None),
        P("leaf"),
        P(AXES, None),
        P(AXES, None),
    )

    def whole(*arrays):
        return local(sizes, *arrays)

    return jax.shard_map(
        whole,
        mesh=mesh,
        in_specs=placed,
        out_specs=(P("leaf", ("row", "col"), None), P(AXES, None)),
        check_vma=False,
    )
```

```python
import functools

import jax
import jax.numpy as jnp
from jax import lax
from jax.experimental import pallas as pl
from jax.experimental.pallas import tpu as pltpu
from jax.sharding import PartitionSpec as P


BF16 = jnp.bfloat16
F32 = jnp.float32
AXES = ("leaf", "row", "col")
FIRST = (((0,), (0,)), ((), ()))
VM = pl.BlockSpec(memory_space=pltpu.VMEM)
SM = pl.BlockSpec(memory_space=pltpu.SMEM)
ANY = pl.BlockSpec(memory_space=pltpu.HBM)


def kernel_call(body, outs, operands, scratch=(), flops=0, vmem=10, apart=()):
    moved = sum(a.size * a.dtype.itemsize for a in operands)
    moved += sum(o.size * o.dtype.itemsize for o in outs)
    specs = [
        ANY if k in apart else SM if a.dtype == jnp.int32 else VM for k, a in enumerate(operands)
    ]
    operands = [
        pltpu.with_memory_space_constraint(a, pltpu.HBM) if k in apart and a.size > 100000 else a
        for k, a in enumerate(operands)
    ]
    return pl.pallas_call(
        body,
        out_shape=list(outs),
        in_specs=specs,
        out_specs=[VM] * len(outs),
        scratch_shapes=list(scratch),
        cost_estimate=pl.CostEstimate(flops=flops, bytes_accessed=moved, transcendentals=0),
        compiler_params=pltpu.CompilerParams(vmem_limit_bytes=vmem << 20),
    )(*operands)


def columns_copy(factor, index, k, target, sem):
    width = target.shape[1]
    start = pl.multiple_of(index[k] * width, width)
    return pltpu.make_async_copy(factor.at[:, pl.ds(start, width)], target, sem)


def load_kernel(count, parts, groups, block, column, factor, separator, *refs):
    wide, cut, sems = refs[:count], refs[count:-1], refs[-1]
    size = separator.shape[0]
    copies = []
    for k in range(parts):
        for g in range(groups):
            start = pl.multiple_of(column[k * groups + g] * size, size)
            copies.append(
                pltpu.make_async_copy(
                    separator.at[:, pl.ds(start, size)],
                    cut[k].at[:, pl.ds(g * size, size)],
                    sems.at[len(copies)],
                )
            )
    for k in range(count):
        copies.append(columns_copy(factor, block, k, wide[k], sems.at[len(copies)]))
    for copy in copies:
        copy.start()
    for copy in copies:
        copy.wait()


def near_kernel(count, far, block, factor, coupling, *refs):
    blocks, pieces = refs[:count], refs[count : 2 * count]
    partial, tall, wide, sems = refs[2 * count], refs[2 * count + 1], refs[2 * count + 2 : -1], refs[-1]
    copies = [
        columns_copy(factor, block, count + k, wide[k], sems.at[k]) for k in range(far)
    ]
    copies.append(
        pltpu.make_async_copy(coupling.at[pl.ds(0, tall.shape[0]), :], tall, sems.at[far])
    )
    for copy in copies:
        copy.start()
    total = None
    for k in range(count):
        term = jnp.dot(blocks[k][...], pieces[k][...], preferred_element_type=F32)
        total = term if total is None else total + term
    partial[...] = total
    for copy in copies:
        copy.wait()


def chunk_of(rows):
    return 256 if rows % 256 == 0 else rows


def update_kernel(groups, far, place_far, coupling, partial, upper, *refs):
    blocks, pieces = refs[:far], refs[far : 2 * far]
    forward, lower, own = refs[2 * far : 2 * far + 3]
    sent = refs[2 * far + 3 : -5]
    place, sems, placed, held = refs[-5], refs[-4], refs[-3], refs[-2:]
    order = placed.shape[0] - 8
    split = upper.shape[0]
    step = chunk_of(split)
    count = (split + lower.shape[0]) // step
    index_copy = pltpu.make_async_copy(place_far, place, sems.at[0])
    lower_copy = pltpu.make_async_copy(
        coupling.at[pl.ds(split, lower.shape[0]), :], lower, sems.at[1]
    )
    index_copy.start()
    lower_copy.start()
    placed[...] = jnp.zeros_like(placed)
    total = partial[...]
    for k in range(far):
        total = total + jnp.dot(blocks[k][...], pieces[k][...], preferred_element_type=F32)
    forward[...] = total.astype(BF16)
    index_copy.wait()

    def multiply(k):
        first = k * step
        if first == split:
            lower_copy.wait()
        source = upper if first < split else lower
        first = first if first < split else first - split
        held[k % 2][...] = jnp.dot(
            source[first : first + step, :], forward[...], preferred_element_type=F32
        )

    def scatter(k):
        for t in range(step):
            placed[pl.ds(place[k * step + t], 1), :] = held[k % 2][t : t + 1, :]

    multiply(0)
    for k in range(count):
        if k + 1 < count:
            multiply(k + 1)
        scatter(k)
    part = order // groups
    own[...] = placed[0:part, :]
    for k, ref in enumerate(sent):
        ref[...] = placed[(k + 1) * part : (k + 2) * part, :].astype(BF16)


def add_kernel(arrived, parts, *refs):
    own, received = refs[0], refs[1 : 1 + arrived]
    kept, sent = refs[1 + arrived], refs[2 + arrived :]
    rows = own.shape[0] // parts
    for k in range(parts):
        span = slice(k * rows, (k + 1) * rows)
        total = own[span, :]
        for ref in received:
            total = total + ref[span, :].astype(F32)
        if k == 0:
            kept[...] = total
        else:
            sent[k - 1][...] = total.astype(BF16)


def gathered_kernel(arrived, *refs):
    rhs, own, received, out = refs[0], refs[1], refs[2 : 2 + arrived], refs[-1]
    total = own[...]
    for ref in received:
        total = total + ref[...].astype(F32)
    out[...] = (rhs[...].astype(F32) - total).astype(BF16)


def finish_kernel(arrived, *refs):
    own, received = refs[0], refs[1 : 1 + arrived]
    total = own[...]
    for ref in received:
        total = total + ref[...].astype(F32)
    refs[-2][...] = total
    refs[-1][...] = total.astype(BF16)


def stack_kernel(*refs):
    out = refs[-1]
    rows = refs[0].shape[0]
    for k, ref in enumerate(refs[:-1]):
        out[k * rows : (k + 1) * rows, :] = ref[...]


def root_forward_kernel(parts, halves, *refs):
    blocks, right = refs[:parts], refs[parts : parts + halves]
    kept, sent = refs[-2], refs[-1]
    rows = blocks[0].shape[0]
    width = right[0].shape[0]
    for k in range(parts):
        total = None
        for h in range(halves):
            term = jnp.dot(
                blocks[k][:, h * width : (h + 1) * width],
                right[h][...],
                preferred_element_type=F32,
            )
            total = term if total is None else total + term
        kept[k * rows : (k + 1) * rows, :] = total
        sent[k * rows : (k + 1) * rows, :] = total.astype(BF16)


def root_back_kernel(parts, halves, sources, *refs):
    blocks, own = refs[:parts], refs[parts]
    received = refs[parts + 1 : 2 * parts]
    outs = refs[2 * parts :]
    rows = blocks[0].shape[0]
    others = [ref[...].astype(F32) for ref in received]
    values = []
    for k in range(parts):
        total = own[k * rows : (k + 1) * rows, :]
        for other, source in zip(others, sources):
            total = total + other[source[k] * rows : (source[k] + 1) * rows, :]
        values.append(total.astype(BF16))
    width = blocks[0].shape[1] // halves
    for h in range(halves):
        total = None
        for k in range(parts):
            term = lax.dot_general(
                blocks[k][:, h * width : (h + 1) * width],
                values[k],
                FIRST,
                preferred_element_type=F32,
            )
            total = term if total is None else total + term
        outs[h][...] = total.astype(outs[h].dtype)


def border_kernel(blocks, far, place_far, forward, upper, lower, *refs):
    wide, pieces = refs[:far], refs[far : far + blocks]
    corrected, sent = refs[far + blocks], refs[far + blocks + 1 : -6]
    place, sem, table, sums, held = refs[-6], refs[-5], refs[-4], refs[-3], refs[-2:]
    index_copy = pltpu.make_async_copy(place_far, place, sem.at[0])
    index_copy.start()
    rows = pieces[0].shape[0]
    order = blocks * rows
    split = upper.shape[0]
    step = chunk_of(split)
    count = (split + lower.shape[0]) // step
    for k in range(blocks):
        table[k * rows : (k + 1) * rows, :] = pieces[k][...].astype(F32)
    table[order : order + 8, :] = jnp.zeros((8, table.shape[1]), F32)
    sums[...] = forward[...].astype(F32).T
    index_copy.wait()

    def gather(k):
        for t in range(step):
            held[k % 2][t : t + 1, :] = table[pl.ds(place[k * step + t], 1), :]

    def multiply(k):
        first = k * step
        source = upper if first < split else lower
        first = first if first < split else first - split
        sums[...] -= lax.dot_general(
            held[k % 2][...].astype(BF16),
            source[first : first + step, :],
            FIRST,
            preferred_element_type=F32,
        )

    gather(0)
    for k in range(count):
        if k + 1 < count:
            gather(k + 1)
        multiply(k)
    corrected[...] = sums[...].astype(BF16)
    for k, ref in enumerate(sent):
        ref[...] = jnp.dot(
            corrected[...], wide[k][...], preferred_element_type=F32
        ).astype(ref.dtype)


def blocks_kernel(corrected, *refs):
    count = len(refs) // 2
    for wide, ref in zip(refs[:count], refs[count:]):
        ref[...] = jnp.dot(
            corrected[...], wide[...], preferred_element_type=F32
        ).astype(ref.dtype)


def sum_kernel(out_dtype, *refs):
    total = refs[0][...].astype(F32)
    for ref in refs[1:-1]:
        total = total + ref[...].astype(F32)
    refs[-1][...] = total.astype(out_dtype)


def last_kernel(*refs):
    total = refs[0][...].astype(F32)
    for ref in refs[1:-1]:
        total = total + ref[...].astype(F32)
    refs[-1][...] = total.T


def like(shape, dtype):
    return jax.ShapeDtypeStruct(tuple(shape), dtype)


def local(
    sizes,
    leaf_rhs,
    leaf_factor,
    leaf_coupling,
    border_rows,
    border_count,
    separator_rhs,
    separator_factor,
):
    nl, nr, nc = sizes
    nx = 2 if nl % 2 == 0 else 1
    nz = nl // nx
    rhs, factor, coupling = leaf_rhs[0], leaf_factor[0], leaf_coupling[0]
    rows, columns = rhs.shape
    borders = coupling.shape[0]
    own_rows, order = separator_factor.shape
    leaf = lax.axis_index("leaf")
    z, x = leaf // nx, leaf % nx
    y, c = lax.axis_index("row"), lax.axis_index("col")
    plane = [(dx, dy) for dx in range(nx) for dy in range(nr)]
    parts = len(plane)
    section = [(dy, dc) for dy in range(nr) for dc in range(nc)]

    def shift(value, dz=0, dx=0, dy=0, dc=0):
        pairs = []
        for a in range(nz):
            for b in range(nx):
                for d in range(nr):
                    for e in range(nc):
                        here = ((a * nx + b) * nr + d) * nc + e
                        a2, b2 = (a + dz) % nz, (b + dx) % nx
                        d2, e2 = (d + dy) % nr, (e + dc) % nc
                        pairs.append((here, ((a2 * nx + b2) * nr + d2) * nc + e2))
        return lax.ppermute(value, AXES, pairs)

    def send_z(values):
        out = []
        for dz in range(1, nz):
            out.append(shift(values[dz], dz=dz))
        return out

    by_row = {0: rhs}
    for dy in range(1, nr):
        by_row[dy] = shift(rhs, dy=-dy)
    pieces = []
    for dy, dc in section:
        pieces.append(by_row[dy] if dc == 0 else shift(by_row[dy], dc=-dc))
    block = jnp.stack([((y + dy) % nr) * nc + (c + dc) % nc for dy, dc in section]).astype(
        jnp.int32
    )

    row = border_rows[0]
    device, inside = row // own_rows, row % own_rows
    rel_c = (device % nc - c) % nc
    rel_y = (device // nc % nr - y) % nr
    rel_x = (device // (nc * nr) % nx - x) % nx
    rel_z = (device // (nc * nr * nx) - z) % nz
    place = (((rel_c * nx + rel_x) * nr + rel_y) * nz + rel_z) * own_rows + inside
    live = jnp.arange(borders, dtype=jnp.int32) < border_count[0]
    place = jnp.where(live, place, order).astype(jnp.int32)

    groups = [(dc, dz) for dc in range(nc) for dz in range(nz)]
    wide = len(groups) * own_rows

    def owner(dx, dy, dz, dc):
        return ((((z + dz) % nz) * nx + (x + dx) % nx) * nr + (y + dy) % nr) * nc + (c + dc) % nc

    direct = own_rows % 128 == 0
    column = jnp.stack(
        [owner(dx, dy, dz, dc) for dx, dy in plane for dc, dz in groups]
    ).astype(jnp.int32)
    loads = parts if direct else 0
    loaded = kernel_call(
        functools.partial(load_kernel, nc, loads, len(groups)),
        [like((rows, rows), BF16)] * nc + [like((own_rows, wide), BF16)] * loads,
        [block, column, factor, separator_factor],
        scratch=[pltpu.SemaphoreType.DMA((nc + loads * len(groups),))],
        apart=(2, 3),
    )
    near_blocks, cut = loaded[:nc], loaded[nc:]
    if not direct:
        cut = [
            jnp.concatenate(
                [
                    lax.dynamic_slice_in_dim(
                        separator_factor, owner(dx, dy, dz, dc) * own_rows, own_rows, 1
                    )
                    for dc, dz in groups
                ],
                1,
            )
            for dx, dy in plane
        ]
    root = [cut[0]]
    held = list(cut)
    late = [plane.index((dx, dy)) for dx, dy in plane if dy > 0]
    if nr > 1:
        *after, pieces[nc] = lax.optimization_barrier((*[cut[k] for k in late], pieces[nc]))
        for k, value in zip(late, after):
            held[k] = value
    for dx, dy in plane[1:]:
        k = plane.index(((-dx) % nx, (-dy) % nr))
        root.append(shift(held[k], dx=-dx, dy=-dy))

    half = order // nc
    far_count = len(section) - nc
    split = borders // 2
    loaded = kernel_call(
        functools.partial(near_kernel, nc, far_count),
        [like((rows, columns), F32), like((split, rows), BF16)]
        + [like((rows, rows), BF16)] * far_count,
        [block, factor, coupling, *near_blocks, *pieces[:nc]],
        scratch=[pltpu.SemaphoreType.DMA((far_count + 1,))],
        flops=2 * rows * rows * nc * columns,
        apart=(1, 2),
    )
    near, upper, far_blocks = loaded[0], loaded[1], loaded[2:]
    outs = kernel_call(
        functools.partial(update_kernel, nc, far_count),
        [
            like((rows, columns), BF16),
            like((borders - split, rows), BF16),
            like((half, columns), F32),
        ]
        + [like((half, columns), BF16)] * (nc - 1),
        [place, coupling, near, upper, *far_blocks, *pieces[nc:]],
        scratch=[
            pltpu.SMEM(place.shape, jnp.int32),
            pltpu.SemaphoreType.DMA((2,)),
            pltpu.VMEM((order + 8, columns), F32),
        ]
        + [pltpu.VMEM((chunk_of(split), columns), F32)] * 2,
        flops=2 * (coupling.size + rows * rows * far_count) * columns,
        apart=(0, 1),
    )
    forward, lower, outs = outs[0], outs[1], outs[2:]
    received = [shift(outs[dc], dc=dc) for dc in range(1, nc)]
    size = half // parts
    outs = kernel_call(
        functools.partial(add_kernel, len(received), parts),
        [like((size, columns), F32)] + [like((size, columns), BF16)] * (parts - 1),
        [outs[0], *received],
    )
    received = []
    for k, (dx, dy) in list(enumerate(plane))[1:]:
        received.append(shift(outs[k], dx=dx, dy=dy))
    outs = kernel_call(
        functools.partial(add_kernel, len(received), nz),
        [like((own_rows, columns), F32)] + [like((own_rows, columns), BF16)] * (nz - 1),
        [outs[0], *received],
    )
    received = send_z(outs)
    gathered = kernel_call(
        functools.partial(gathered_kernel, len(received)),
        [like((own_rows, columns), BF16)],
        [separator_rhs, outs[0], *received],
    )[0]

    def along_z(value):
        values = [value]
        for dz in range(1, nz):
            values.append(shift(value, dz=-dz))
        return kernel_call(stack_kernel, [like((nz * own_rows, columns), BF16)], values)[0]

    column_block = along_z(gathered)
    right = [column_block] + [shift(column_block, dc=-dc) for dc in range(1, nc)]
    kept, sent = kernel_call(
        functools.partial(root_forward_kernel, parts, nc),
        [like((parts * own_rows, columns), F32), like((parts * own_rows, columns), BF16)],
        [*root, *right],
        flops=2 * parts * own_rows * wide * columns,
    )
    received, sources = [], []
    for k, (dx, dy) in list(enumerate(plane))[1:]:
        received.append(shift(sent, dx=-dx, dy=-dy))
        sources.append([plane.index(((px - dx) % nx, (py - dy) % nr)) for px, py in plane])
    outs = kernel_call(
        functools.partial(root_back_kernel, parts, nc, sources),
        [like((nz * own_rows, columns), F32)] + [like((nz * own_rows, columns), BF16)] * (nc - 1),
        [*root, kept, *received],
        flops=2 * parts * own_rows * wide * columns,
    )
    received = [shift(outs[dc], dc=dc) for dc in range(1, nc)]
    outs = kernel_call(
        functools.partial(add_kernel, len(received), nz),
        [like((own_rows, columns), F32)] + [like((own_rows, columns), BF16)] * (nz - 1),
        [outs[0], *received],
    )
    received = send_z(outs)
    separator_solution, rounded = kernel_call(
        functools.partial(finish_kernel, len(received)),
        [like((own_rows, columns), F32), like((own_rows, columns), BF16)],
        [outs[0], *received],
    )
    layer = along_z(rounded)
    table = [layer]
    for k, (dx, dy) in list(enumerate(plane))[1:]:
        table.append(shift(layer, dx=-dx, dy=-dy))
    pieces = list(table)
    for dc in range(1, nc):
        pieces += [shift(value, dc=-dc) for value in table]

    far = [(dy, dc) for dy, dc in section if dy > 0]
    near = [(dy, dc) for dy, dc in section if dy == 0]
    outs = kernel_call(
        functools.partial(border_kernel, len(pieces), len(far)),
        [like((columns, rows), BF16)]
        + [like((columns, rows), F32 if dc == 0 else BF16) for dy, dc in far],
        [place, forward, upper, lower, *far_blocks, *pieces],
        scratch=[
            pltpu.SMEM(place.shape, jnp.int32),
            pltpu.SemaphoreType.DMA((1,)),
            pltpu.VMEM((order + 8, columns), F32),
            pltpu.VMEM((columns, rows), F32),
        ]
        + [pltpu.VMEM((chunk_of(split), columns), F32)] * 2,
        flops=2 * (coupling.size + factor.size * len(far) // len(section)) * columns,
        apart=(0,),
    )
    corrected, far_parts = outs[0], dict(zip(far, outs[1:]))
    arrived = []
    for dy in range(1, nr):
        terms = [far_parts[dy, 0]] + [shift(far_parts[dy, dc], dc=dc) for dc in range(1, nc)]
        total = kernel_call(
            functools.partial(sum_kernel, BF16), [like((columns, rows), BF16)], terms
        )[0]
        arrived.append(shift(total, dy=dy))
    outs = kernel_call(
        blocks_kernel,
        [like((columns, rows), F32 if dc == 0 else BF16) for dy, dc in near],
        [corrected, *near_blocks],
        flops=2 * factor.size * len(near) // len(section) * columns,
    )
    terms = [outs[0]] + [shift(outs[dc], dc=dc) for dc in range(1, nc)]
    leaf_solution = kernel_call(last_kernel, [like((rows, columns), F32)], [*terms, *arrived])[0]
    return leaf_solution[None], separator_solution


def solution(mesh):
    sizes = tuple(mesh.shape[name] for name in AXES)
    placed = (
        P("leaf", ("row", "col"), None),
        P("leaf", ("row", "col"), None),
        P("leaf", None, ("row", "col")),
        P("leaf", None),
        P("leaf"),
        P(AXES, None),
        P(AXES, None),
    )

    def whole(*arrays):
        return local(sizes, *arrays)

    return jax.shard_map(
        whole,
        mesh=mesh,
        in_specs=placed,
        out_specs=(P("leaf", ("row", "col"), None), P(AXES, None)),
        check_vma=False,
    )
```

```python
import functools

import jax
import jax.numpy as jnp
from jax import lax
from jax.experimental import pallas as pl
from jax.experimental.pallas import tpu as pltpu
from jax.sharding import PartitionSpec as P


BF16 = jnp.bfloat16
F32 = jnp.float32
AXES = ("leaf", "row", "col")
FIRST = (((0,), (0,)), ((), ()))
VM = pl.BlockSpec(memory_space=pltpu.VMEM)
SM = pl.BlockSpec(memory_space=pltpu.SMEM)
ANY = pl.BlockSpec(memory_space=pltpu.HBM)


def kernel_call(body, outs, operands, scratch=(), flops=0, vmem=10, name=None, apart=(), vector=()):
    moved = sum(a.size * a.dtype.itemsize for a in operands)
    moved += sum(o.size * o.dtype.itemsize for o in outs)
    specs = [
        ANY if k in apart else SM if a.dtype == jnp.int32 and k not in vector else VM
        for k, a in enumerate(operands)
    ]
    operands = [
        pltpu.with_memory_space_constraint(a, pltpu.HBM) if k in apart and name == "near" else a
        for k, a in enumerate(operands)
    ]
    return pl.pallas_call(
        body,
        out_shape=list(outs),
        in_specs=specs,
        out_specs=[VM] * len(outs),
        scratch_shapes=list(scratch),
        cost_estimate=pl.CostEstimate(flops=flops, bytes_accessed=moved, transcendentals=0),
        compiler_params=pltpu.CompilerParams(vmem_limit_bytes=vmem << 20),
    )(*operands)


def columns_copy(factor, index, k, target, sem):
    width = target.shape[1]
    start = pl.multiple_of(index[k] * width, width)
    return pltpu.make_async_copy(factor.at[:, pl.ds(start, width)], target, sem)


def quotient(value, size):
    return value >> (size.bit_length() - 1) if size & (size - 1) == 0 else value // size


def remainder(value, size):
    return value & (size - 1) if size & (size - 1) == 0 else lax.rem(value, size)


def near_kernel(
    sizes,
    count,
    far,
    parts,
    groups,
    block,
    column,
    here,
    factor,
    separator,
    border,
    coupling,
    rhs,
    *refs,
):
    pieces, refs = refs[: count - 1], refs[count - 1 :]
    partial, place, tall, refs = refs[0], refs[1], refs[2], refs[3:]
    wide, cut = refs[: count + far], refs[count + far : -3]
    rows_held, rhs_held, sems = refs[-3], refs[-2], refs[-1]
    pieces = (rhs_held, *pieces)
    size = separator.shape[0]
    copies = [columns_copy(factor, block, k, wide[k], sems.at[k]) for k in range(count + far)]
    rest = [pltpu.make_async_copy(border, rows_held, sems.at[count + far])]
    for k in range(parts):
        for g in range(groups):
            start = pl.multiple_of(column[k * groups + g] * size, size)
            rest.append(
                pltpu.make_async_copy(
                    separator.at[:, pl.ds(start, size)],
                    cut[k].at[:, pl.ds(g * size, size)],
                    sems.at[count + far + len(rest)],
                )
            )
    early = pltpu.make_async_copy(rhs, rhs_held, sems.at[count + far + len(rest)])
    late = pltpu.make_async_copy(coupling, tall, sems.at[count + far + len(rest) + 1])
    for copy in [early] + copies[:count] + rest:
        copy.start()
    early.wait()
    total = None
    for k in range(count):
        copies[k].wait()
        if k == 0:
            for copy in copies[count:] + [late]:
                copy.start()
        term = jnp.dot(wide[k][...], pieces[k][...], preferred_element_type=F32)
        total = term if total is None else total + term
    partial[...] = total
    rest[0].wait()
    row = rows_held[...]
    device, inside = quotient(row, size), remainder(row, size)
    digits = []
    for axis in range(3):
        length = sizes[axis]
        digits.append(remainder(remainder(device, length) - here[axis] + length, length))
        device = quotient(device, length)
    digits.append(remainder(device - here[3] + sizes[3], sizes[3]))
    first = digits[0]
    for axis in (2, 1, 3):
        first = first * sizes[axis] + digits[axis]
    position = lax.broadcasted_iota(jnp.int32, row.shape, 0) * row.shape[1]
    position = position + lax.broadcasted_iota(jnp.int32, row.shape, 1)
    order = size * sizes[0] * sizes[1] * sizes[2] * sizes[3]
    place[...] = jnp.where(position < here[4], first * size + inside, order)
    for copy in rest[1:] + copies[count:] + [late]:
        copy.wait()


def chunk_of(rows):
    return 256 if rows % 256 == 0 else rows


def update_kernel(groups, far, place_far, tall, partial, *refs):
    blocks, pieces = refs[:far], refs[far : 2 * far]
    forward, own, sent = refs[2 * far], refs[2 * far + 1], refs[2 * far + 2 : -5]
    place, sems, placed, held = refs[-5], refs[-4], refs[-3], refs[-2:]
    order = placed.shape[0] - 8
    step = chunk_of(tall.shape[0])
    count = tall.shape[0] // step
    index_copy = pltpu.make_async_copy(place_far, place, sems.at[0])
    index_copy.start()
    placed[...] = jnp.zeros_like(placed)
    total = partial[...]
    for k in range(far):
        total = total + jnp.dot(blocks[k][...], pieces[k][...], preferred_element_type=F32)
    forward[...] = total.astype(BF16)
    index_copy.wait()

    def multiply(k):
        held[k % 2][...] = jnp.dot(
            tall[k * step : (k + 1) * step, :], forward[...], preferred_element_type=F32
        )

    lanes = place.shape[1]

    def scatter(k):
        for t in range(k * step, (k + 1) * step):
            row = place[t // lanes, t % lanes]
            placed[pl.ds(row, 1), :] = held[k % 2][t - k * step : t - k * step + 1, :]

    multiply(0)
    for k in range(count):
        if k + 1 < count:
            multiply(k + 1)
        scatter(k)
    part = order // groups
    own[...] = placed[0:part, :]
    for k, ref in enumerate(sent):
        ref[...] = placed[(k + 1) * part : (k + 2) * part, :].astype(BF16)


def add_kernel(arrived, parts, *refs):
    own, received = refs[0], refs[1 : 1 + arrived]
    kept, sent = refs[1 + arrived], refs[2 + arrived :]
    rows = own.shape[0] // parts
    for k in range(parts):
        span = slice(k * rows, (k + 1) * rows)
        total = own[span, :]
        for ref in received:
            total = total + ref[span, :].astype(F32)
        if k == 0:
            kept[...] = total
        else:
            sent[k - 1][...] = total.astype(BF16)


def gathered_kernel(arrived, *refs):
    rhs, own, received, out = refs[0], refs[1], refs[2 : 2 + arrived], refs[-1]
    total = own[...]
    for ref in received:
        total = total + ref[...].astype(F32)
    out[...] = (rhs[...].astype(F32) - total).astype(BF16)


def finish_kernel(arrived, *refs):
    own, received = refs[0], refs[1 : 1 + arrived]
    total = own[...]
    for ref in received:
        total = total + ref[...].astype(F32)
    refs[-1][...] = total.astype(refs[-1].dtype)


def stack_kernel(*refs):
    out = refs[-1]
    rows = refs[0].shape[0]
    for k, ref in enumerate(refs[:-1]):
        out[k * rows : (k + 1) * rows, :] = ref[...]


def root_forward_kernel(parts, halves, *refs):
    blocks, right = refs[:parts], refs[parts : parts + halves]
    kept, sent = refs[-2], refs[-1]
    rows = blocks[0].shape[0]
    width = right[0].shape[0]
    for k in range(parts):
        total = None
        for h in range(halves):
            term = jnp.dot(
                blocks[k][:, h * width : (h + 1) * width],
                right[h][...],
                preferred_element_type=F32,
            )
            total = term if total is None else total + term
        kept[k * rows : (k + 1) * rows, :] = total
        sent[k * rows : (k + 1) * rows, :] = total.astype(BF16)


def root_back_kernel(parts, halves, sources, *refs):
    blocks, own = refs[:parts], refs[parts]
    received = refs[parts + 1 : 2 * parts]
    outs = refs[2 * parts :]
    rows = blocks[0].shape[0]
    others = [ref[...].astype(F32) for ref in received]
    values = []
    for k in range(parts):
        total = own[k * rows : (k + 1) * rows, :]
        for other, source in zip(others, sources):
            total = total + other[source[k] * rows : (source[k] + 1) * rows, :]
        values.append(total.astype(BF16))
    width = blocks[0].shape[1] // halves
    for h in range(halves):
        total = None
        for k in range(parts):
            term = lax.dot_general(
                blocks[k][:, h * width : (h + 1) * width],
                values[k],
                FIRST,
                preferred_element_type=F32,
            )
            total = term if total is None else total + term
        outs[h][...] = total.astype(outs[h].dtype)


def border_kernel(blocks, far, place_far, forward, tall, *refs):
    wide, pieces = refs[:far], refs[far : far + blocks]
    corrected, sent = refs[far + blocks], refs[far + blocks + 1 : -6]
    place, sem, table, sums, held = refs[-6], refs[-5], refs[-4], refs[-3], refs[-2:]
    index_copy = pltpu.make_async_copy(place_far, place, sem.at[0])
    index_copy.start()
    rows = pieces[0].shape[0]
    order = blocks * rows
    step = chunk_of(tall.shape[0])
    count = tall.shape[0] // step
    lanes = place.shape[1]
    for k in range(blocks):
        table[k * rows : (k + 1) * rows, :] = pieces[k][...].astype(F32)
    table[order : order + 8, :] = jnp.zeros((8, table.shape[1]), F32)
    sums[...] = forward[...].astype(F32).T
    index_copy.wait()

    def gather(k):
        for t in range(k * step, (k + 1) * step):
            row = place[t // lanes, t % lanes]
            held[k % 2][t - k * step : t - k * step + 1, :] = table[pl.ds(row, 1), :]

    def multiply(k):
        sums[...] -= lax.dot_general(
            held[k % 2][...].astype(BF16),
            tall[k * step : (k + 1) * step, :],
            FIRST,
            preferred_element_type=F32,
        )

    gather(0)
    for k in range(count):
        if k + 1 < count:
            gather(k + 1)
        multiply(k)
    corrected[...] = sums[...].astype(BF16)
    for k, ref in enumerate(sent):
        ref[...] = jnp.dot(
            corrected[...], wide[k][...], preferred_element_type=F32
        ).astype(ref.dtype)


def blocks_kernel(corrected, *refs):
    count = len(refs) // 2
    for wide, ref in zip(refs[:count], refs[count:]):
        ref[...] = jnp.dot(
            corrected[...], wide[...], preferred_element_type=F32
        ).astype(ref.dtype)


def sum_kernel(out_dtype, *refs):
    total = refs[0][...].astype(F32)
    for ref in refs[1:-1]:
        total = total + ref[...].astype(F32)
    refs[-1][...] = total.astype(out_dtype)


def turn_kernel(*refs):
    total = refs[0][...].astype(F32)
    for ref in refs[1:-1]:
        total = total + ref[...].astype(F32)
    refs[-1][...] = total.T


def last_kernel(kept, *refs):
    total = refs[0][...].astype(F32)
    for ref in refs[1:-1]:
        total = total + ref[...].astype(F32)
    refs[-1][...] = kept[...] + total.T


def like(shape, dtype):
    return jax.ShapeDtypeStruct(tuple(shape), dtype)


def local(
    sizes,
    leaf_rhs,
    leaf_factor,
    leaf_coupling,
    border_rows,
    border_count,
    separator_rhs,
    separator_factor,
):
    nl, nr, nc = sizes
    nx = 2 if nl % 2 == 0 else 1
    nz = nl // nx
    rhs, factor, coupling = leaf_rhs[0], leaf_factor[0], leaf_coupling[0]
    rows, columns = rhs.shape
    borders = coupling.shape[0]
    own_rows, order = separator_factor.shape
    leaf = lax.axis_index("leaf")
    z, x = leaf // nx, leaf % nx
    y, c = lax.axis_index("row"), lax.axis_index("col")
    plane = [(dx, dy) for dx in range(nx) for dy in range(nr)]
    parts = len(plane)
    section = [(dy, dc) for dy in range(nr) for dc in range(nc)]

    def shift(value, dz=0, dx=0, dy=0, dc=0):
        pairs = []
        for a in range(nz):
            for b in range(nx):
                for d in range(nr):
                    for e in range(nc):
                        here = ((a * nx + b) * nr + d) * nc + e
                        a2, b2 = (a + dz) % nz, (b + dx) % nx
                        d2, e2 = (d + dy) % nr, (e + dc) % nc
                        pairs.append((here, ((a2 * nx + b2) * nr + d2) * nc + e2))
        return lax.ppermute(value, AXES, pairs)

    def send_z(values):
        out = []
        for dz in range(1, nz):
            out.append(shift(values[dz], dz=dz))
        return out

    by_row = {0: rhs}
    for dy in range(1, nr):
        by_row[dy] = shift(rhs, dy=-dy)
    pieces = []
    for dy, dc in section:
        pieces.append(by_row[dy] if dc == 0 else shift(by_row[dy], dc=-dc))
    block = jnp.stack([((y + dy) % nr) * nc + (c + dc) % nc for dy, dc in section]).astype(
        jnp.int32
    )

    here = jnp.stack([c, y, x, z, border_count[0]]).astype(jnp.int32)
    border = border_rows.reshape(borders // 128, 128) if borders % 128 == 0 else border_rows

    groups = [(dc, dz) for dc in range(nc) for dz in range(nz)]
    wide = len(groups) * own_rows

    def owner(dx, dy, dz, dc):
        return ((((z + dz) % nz) * nx + (x + dx) % nx) * nr + (y + dy) % nr) * nc + (c + dc) % nc

    direct = own_rows % 128 == 0
    column = jnp.stack(
        [owner(dx, dy, dz, dc) for dx, dy in plane for dc, dz in groups]
    ).astype(jnp.int32)
    loads = parts if direct else 0
    far_count = len(section) - nc
    loaded = kernel_call(
        functools.partial(
            near_kernel, (nc, nr, nx, nz), nc, far_count, loads, len(groups)
        ),
        [
            like((rows, columns), F32),
            like(border.shape, jnp.int32),
            like(coupling.shape, BF16),
        ]
        + [like((rows, rows), BF16)] * len(section)
        + [like((own_rows, wide), BF16)] * loads,
        [block, column, here, factor, separator_factor, border, coupling, *pieces[:nc]],
        scratch=[
            pltpu.VMEM(border.shape, jnp.int32),
            pltpu.VMEM(rhs.shape, BF16),
            pltpu.SemaphoreType.DMA((len(section) + loads * len(groups) + 3,)),
        ],
        flops=2 * rows * rows * nc * columns,
        name="near",
        apart=(3, 4, 5, 6, 7),
    )
    near, place, tall, near_blocks = *loaded[:3], loaded[3 : 3 + nc]
    far_blocks, cut = loaded[3 + nc : 3 + len(section)], loaded[3 + len(section) :]
    if not direct:
        cut = [
            jnp.concatenate(
                [
                    lax.dynamic_slice_in_dim(
                        separator_factor, owner(dx, dy, dz, dc) * own_rows, own_rows, 1
                    )
                    for dc, dz in groups
                ],
                1,
            )
            for dx, dy in plane
        ]
    root = [cut[0]]
    held = list(cut)
    late = [plane.index((dx, dy)) for dx, dy in plane if dy > 0]
    if nr > 1:
        *after, pieces[nc] = lax.optimization_barrier((*[cut[k] for k in late], pieces[nc]))
        for k, value in zip(late, after):
            held[k] = value
    for dx, dy in plane[1:]:
        k = plane.index(((-dx) % nx, (-dy) % nr))
        root.append(shift(held[k], dx=-dx, dy=-dy))

    half = order // nc
    outs = kernel_call(
        functools.partial(update_kernel, nc, far_count),
        [
            like((rows, columns), BF16),
            like((half, columns), F32),
        ]
        + [like((half, columns), BF16)] * (nc - 1),
        [place, tall, near, *far_blocks, *pieces[nc:]],
        scratch=[
            pltpu.SMEM(place.shape, jnp.int32),
            pltpu.SemaphoreType.DMA((1,)),
            pltpu.VMEM((order + 8, columns), F32),
        ]
        + [pltpu.VMEM((chunk_of(borders), columns), F32)] * 2,
        flops=2 * (coupling.size + rows * rows * far_count) * columns,
        name="update",
        apart=(0,),
    )
    forward, outs = outs[0], outs[1:]
    received = [shift(outs[dc], dc=dc) for dc in range(1, nc)]
    size = half // parts
    outs = kernel_call(
        functools.partial(add_kernel, len(received), parts),
        [like((size, columns), F32)] + [like((size, columns), BF16)] * (parts - 1),
        [outs[0], *received],
        name="add_col",
    )
    received = []
    for k, (dx, dy) in list(enumerate(plane))[1:]:
        received.append(shift(outs[k], dx=dx, dy=dy))
    outs = kernel_call(
        functools.partial(add_kernel, len(received), nz),
        [like((own_rows, columns), F32)] + [like((own_rows, columns), BF16)] * (nz - 1),
        [outs[0], *received],
        name="add_plane",
    )
    received = send_z(outs)
    gathered = kernel_call(
        functools.partial(gathered_kernel, len(received)),
        [like((own_rows, columns), BF16)],
        [separator_rhs, outs[0], *received],
        name="gathered",
    )[0]

    def along_z(value):
        values = [value]
        for dz in range(1, nz):
            values.append(shift(value, dz=-dz))
        return kernel_call(
            stack_kernel, [like((nz * own_rows, columns), BF16)], values, name="stack"
        )[0]

    column_block = along_z(gathered)
    right = [column_block] + [shift(column_block, dc=-dc) for dc in range(1, nc)]
    kept, sent = kernel_call(
        functools.partial(root_forward_kernel, parts, nc),
        [like((parts * own_rows, columns), F32), like((parts * own_rows, columns), BF16)],
        [*root, *right],
        flops=2 * parts * own_rows * wide * columns,
        name="root_forward",
    )
    received, sources = [], []
    for k, (dx, dy) in list(enumerate(plane))[1:]:
        received.append(shift(sent, dx=-dx, dy=-dy))
        sources.append([plane.index(((px - dx) % nx, (py - dy) % nr)) for px, py in plane])
    outs = kernel_call(
        functools.partial(root_back_kernel, parts, nc, sources),
        [like((nz * own_rows, columns), F32)] + [like((nz * own_rows, columns), BF16)] * (nc - 1),
        [*root, kept, *received],
        flops=2 * parts * own_rows * wide * columns,
        name="root_back",
    )
    received = [shift(outs[dc], dc=dc) for dc in range(1, nc)]
    outs = kernel_call(
        functools.partial(add_kernel, len(received), nz),
        [like((own_rows, columns), F32)] + [like((own_rows, columns), BF16)] * (nz - 1),
        [outs[0], *received],
        name="add_col2",
    )
    received = send_z(outs)
    rounded = kernel_call(
        functools.partial(finish_kernel, len(received)),
        [like((own_rows, columns), BF16)],
        [outs[0], *received],
        name="finish",
    )[0]
    separator_solution = kernel_call(
        functools.partial(finish_kernel, len(received)),
        [like((own_rows, columns), F32)],
        [outs[0], *received],
        name="exact",
    )[0]
    layer = along_z(rounded)
    table = [layer]
    for k, (dx, dy) in list(enumerate(plane))[1:]:
        table.append(shift(layer, dx=-dx, dy=-dy))
    pieces = list(table)
    for dc in range(1, nc):
        pieces += [shift(value, dc=-dc) for value in table]

    far = [(dy, dc) for dy, dc in section if dy > 0]
    near = [(dy, dc) for dy, dc in section if dy == 0]
    outs = kernel_call(
        functools.partial(border_kernel, len(pieces), len(far)),
        [like((columns, rows), BF16)]
        + [like((columns, rows), F32 if dc == 0 else BF16) for dy, dc in far],
        [place, forward, tall, *far_blocks, *pieces],
        scratch=[
            pltpu.SMEM(place.shape, jnp.int32),
            pltpu.SemaphoreType.DMA((1,)),
            pltpu.VMEM((order + 8, columns), F32),
            pltpu.VMEM((columns, rows), F32),
        ]
        + [pltpu.VMEM((chunk_of(borders), columns), F32)] * 2,
        flops=2 * (coupling.size + factor.size * len(far) // len(section)) * columns,
        name="border",
        apart=(0,),
    )
    corrected, far_parts = outs[0], dict(zip(far, outs[1:]))
    arrived = []
    for dy in range(1, nr):
        terms = [far_parts[dy, 0]] + [shift(far_parts[dy, dc], dc=dc) for dc in range(1, nc)]
        total = kernel_call(
            functools.partial(sum_kernel, BF16), [like((columns, rows), BF16)], terms, name="sum_far"
        )[0]
        arrived.append(shift(total, dy=dy))
    outs = kernel_call(
        blocks_kernel,
        [like((columns, rows), F32 if dc == 0 else BF16) for dy, dc in near],
        [corrected, *near_blocks],
        flops=2 * factor.size * len(near) // len(section) * columns,
        name="own_blocks",
    )
    terms = [outs[0]] + [shift(outs[dc], dc=dc) for dc in range(1, nc)]
    leaf_solution = kernel_call(turn_kernel, [like((rows, columns), F32)], terms, name="turn")[0]
    if arrived:
        leaf_solution = kernel_call(
            last_kernel, [like((rows, columns), F32)], [leaf_solution, *arrived], name="last"
        )[0]
    return leaf_solution[None], separator_solution


def solution(mesh):
    sizes = tuple(mesh.shape[name] for name in AXES)
    placed = (
        P("leaf", ("row", "col"), None),
        P("leaf", ("row", "col"), None),
        P("leaf", None, ("row", "col")),
        P("leaf", None),
        P("leaf"),
        P(AXES, None),
        P(AXES, None),
    )

    def whole(*arrays):
        return local(sizes, *arrays)

    return jax.shard_map(
        whole,
        mesh=mesh,
        in_specs=placed,
        out_specs=(P("leaf", ("row", "col"), None), P(AXES, None)),
        check_vma=False,
    )
```
